32 devices in a mesh: groups: 2 (over y), strip: 4 (over z), section: 2 (over x), col: 2 (over core).
Axes of the slice: x: 2, y: 2, z: 4, core: 2. Of those that a mesh axis runs over, the one named last changes fastest.
Arguments:
- x_in: float32 [8, 512, 16, 256], P('groups', None, 'strip', 'col'), parts along dimension 0, may hold values from -6 to 6
- w_reduce: float32 [2, 128, 512], P('section'), may hold values from -0.25 to 0.25
- w_spatial: float32 [2, 9, 128, 128], P('section'), may hold values from -0.1875 to 0.1875
- w_expand: float32 [2, 512, 128], P('section'), may hold values from -0.5 to 0.5
- gain_mid: float32 [2, 2, 128], P('section'), may hold values from 0.1 to 1.9
- bias_mid: float32 [2, 2, 128], P('section'), may hold values from -3 to 3
- gain_out: float32 [2, 512], P('section'), may hold values from 0.1 to 1.9
- bias_out: float32 [2, 512], P('section'), may hold values from -3 to 3
Outputs:
- features: float32 [2, 8, 512, 16, 256], P('section', 'groups', None, 'strip', 'col'), parts along dimension 1
The draws below stay inside these ranges and needn't reach their ends.
There are 2 independent parts, one for each index of `groups`. The reference program is written for one: setup_inputs(seed, part) draws one part's arguments, and reference() takes and returns one part's arrays. A program takes and returns all parts, laid end to end along the dimension named above; an argument that names none is the same for every part. Nothing has to cross between parts.
All inputs are finite; a program needn't handle non-finite values.
Results may differ from the reference program's by a relative error of at most 0.00015.
Values sent between devices are 32-bit elements; how exact they have to be, the bound alone decides.
A program may use at most 64 MiB of HBM per device.

```python
import jax
import jax.numpy as jnp
from jax import lax

C = 512
CM = 128
MB = 4
BLOCKS = 2
H = 16
W = 256


def block_levels(key, shape, cuts, low, high):
    factor_of, own = 1.0, jax.random.fold_in(key, 6)
    for axis_at, parts in cuts:
        heights = jnp.exp(jax.random.uniform(jax.random.fold_in(own, axis_at), (parts,), jnp.float32, low / len(cuts), high / len(cuts)))
        factor_of = factor_of * jnp.repeat(heights, shape[axis_at] // parts).reshape([-1 if axis == axis_at else 1 for axis in range(len(shape))])
    return factor_of


def centred(own_key, dims, spread, reach, split=(), dtype=jnp.bfloat16):
    factor_of = block_levels(own_key, dims, split, -0.22, 0.18) if split else 1.0
    drawn = jax.random.normal(own_key, dims, jnp.float32) * spread * factor_of
    return jnp.minimum(jnp.maximum(drawn, -reach), reach).astype(dtype)


def setup_inputs(seed: int = 0, part: int = 0) -> dict:
    key_of = jax.random.split(jax.random.key(seed), 9)
    part_keys = jax.random.split(jax.random.fold_in(key_of[8], part), 9)
    return {
        "x_in": centred(part_keys[0], (MB, C, H, W), 1.0, 6.0, ((2, 4), (3, 2)), jnp.float32),
        "w_reduce": centred(key_of[1], (BLOCKS, CM, C), C ** -0.5, 0.25, ((0, 2),), jnp.float32),
        "w_spatial": centred(key_of[2], (BLOCKS, 9, CM, CM), (9 * CM) ** -0.5, 0.1875, ((0, 2),), jnp.float32),
        "w_expand": centred(key_of[3], (BLOCKS, C, CM), CM ** -0.5, 0.5, ((0, 2),), jnp.float32),
        "gain_mid": jnp.clip(1.0 + 0.18 * jax.random.normal(key_of[4], (BLOCKS, 2, CM), jnp.float32), 0.1, 1.9),
        "bias_mid": centred(key_of[5], (BLOCKS, 2, CM), 0.5, 3.0, ((0, 2),), jnp.float32),
        "gain_out": jnp.clip(1.0 + 0.18 * jax.random.normal(key_of[6], (BLOCKS, C), jnp.float32), 0.1, 1.9),
        "bias_out": centred(key_of[7], (BLOCKS, C), 0.5, 3.0, ((0, 2),), jnp.float32),
    }


def project(weight, field):
    return jnp.einsum("oc,chw->ohw", weight, field, precision=lax.Precision.HIGHEST)


def column(vector):
    return vector[:, None, None]


def bottleneck(image, w_reduce, w_spatial, w_expand, gain_mid, bias_mid, gain_out, bias_out):
    reduced = jax.nn.relu(column(gain_mid[0]) * project(w_reduce, image) + column(bias_mid[0]))
    padded = jnp.pad(reduced, ((0, 0), (1, 1), (1, 1)))
    spatial = jnp.zeros((CM, H, W), jnp.float32)
    for tap in range(9):
        row_off = tap // 3
        col_off = tap % 3
        spatial = spatial + project(w_spatial[tap], padded[:, row_off:row_off + H, col_off:col_off + W])
    middle = jax.nn.relu(column(gain_mid[1]) * spatial + column(bias_mid[1]))
    return jax.nn.relu(image + column(gain_out) * project(w_expand, middle) + column(bias_out))


def reference(x_in, w_reduce, w_spatial, w_expand, gain_mid, bias_mid, gain_out, bias_out):
    def run_tile(image):
        outputs = []
        current = image
        for level in range(BLOCKS):
            current = bottleneck(current, w_reduce[level], w_spatial[level], w_expand[level],
                                 gain_mid[level], bias_mid[level], gain_out[level], bias_out[level])
            outputs.append(current)
        return jnp.stack(outputs)

    per_tile = lax.map(run_tile, x_in)
    return jnp.transpose(per_tile, (1, 0, 2, 3, 4))
```

```python
import functools

import jax
import jax.numpy as jnp
from jax import lax
from jax.experimental import pallas as pl
from jax.experimental.pallas import tpu as pltpu
from jax.sharding import PartitionSpec as P

BF = jnp.bfloat16
F32 = jnp.float32


def split(value):
    high = value.astype(BF)
    return high, (value - high.astype(F32)).astype(BF)


def dot(a, b):
    return jnp.dot(a, b, preferred_element_type=F32)


def down_rows(row, size):
    return jnp.transpose(jnp.broadcast_to(row, (size, size)))


def kernel(
    levels, strips, rows,
    x_ref, wr_ref, ws_ref, wx_ref, pp_ref, out_ref,
    cur, wr_all, ws_all, wx_all, pp_all, red, side, halo, relay,
    w_red, w_spa, w_exp, b_red, b_mid, b_out, sa,
    x_sem, own_sem, wsend, wrecv, rsend, rrecv, hsend, hrecv, nsend, nrecv, ysend, yrecv, out_sem,
):
    tiles = x_ref.shape[0]
    chans = x_ref.shape[1] // rows
    cols = x_ref.shape[2]
    mid = wr_ref.shape[0]
    strip = lax.axis_index("strip")
    sec = lax.axis_index("section")
    col = lax.axis_index("col")
    other = {"col": 1 - col}
    srcs = (wr_ref, ws_ref, wx_ref, pp_ref)
    slots = (wr_all, ws_all, wx_all, pp_all)

    def share(kind, level, which):
        if kind == 0:
            return wr_all.at[level, pl.ds(which * (mid // 2), mid // 2), :]
        if kind == 1:
            return ws_all.at[level, :, pl.ds(which * (mid // 2), mid // 2), :]
        if kind == 2:
            return wx_all.at[level, pl.ds(which * (chans // 2), chans // 2), :]
        return pp_all.at[level]

    def remote(src, dst, send, recv, device):
        return pltpu.make_async_remote_copy(
            src_ref=src, dst_ref=dst, send_sem=send, recv_sem=recv,
            device_id=device, device_id_type=pl.DeviceIdType.MESH,
        )

    own = [
        pltpu.make_async_copy(srcs[k], slots[k].at[sec], own_sem.at[k]) for k in range(4)
    ]
    loads = [
        pltpu.make_async_copy(x_ref.at[m], cur.at[m], x_sem.at[m]) for m in range(tiles)
    ]
    for copy in (own[3], own[0], own[1], own[2]):
        copy.start()
    for copy in loads:
        copy.start()

    barrier = pltpu.get_barrier_semaphore()
    pl.semaphore_signal(barrier, inc=1, device_id=other, device_id_type=pl.DeviceIdType.MESH)
    for step in range(1, levels):
        pl.semaphore_signal(
            barrier, inc=1, device_id={"section": lax.rem(sec + step, levels)},
            device_id_type=pl.DeviceIdType.MESH,
        )

    for there, peer in ((strip > 0, strip - 1), (strip < strips - 1, strip + 1)):
        @pl.when(there)
        def _(peer=peer):
            pl.semaphore_signal(
                barrier, inc=1, device_id={"strip": peer}, device_id_type=pl.DeviceIdType.MESH
            )

    peers = levels + jnp.where(strip > 0, 1, 0) + jnp.where(strip < strips - 1, 1, 0)
    pl.semaphore_wait(barrier, peers)

    for k in (3, 0, 1, 2):
        own[k].wait()
        for target in range(1, levels):
            @pl.when(sec < target)
            def _(k=k, target=target):
                part = share(k, sec, col)
                remote(part, part, wsend.at[k, target], wrecv.at[k, sec], {"section": target}).start()

    @pl.when(strip == 0)
    def _():
        halo[:, :, 0] = jnp.zeros(halo.shape[:2] + halo.shape[3:], F32)
        relay[:, :, 0] = jnp.zeros(relay.shape[:2] + relay.shape[3:], F32)

    @pl.when(strip == strips - 1)
    def _():
        halo[:, :, 1] = jnp.zeros(halo.shape[:2] + halo.shape[3:], F32)
        relay[:, :, 1] = jnp.zeros(relay.shape[:2] + relay.shape[3:], F32)

    def relayed(k, level, which):
        part = share(k, level, which)
        return remote(part, part, rsend.at[k, level], rrecv.at[k, level], other)

    def arrive(level, kinds):
        @pl.when(sec > level)
        def _():
            for k in kinds:
                part = share(k, level, col)
                remote(part, part, wsend.at[k, 0], wrecv.at[k, level], other).wait_recv()
                if k < 3:
                    relayed(k, level, col).start()
            for k in kinds:
                if k < 3:
                    relayed(k, level, 1 - col).wait_recv()

    def prepare_reduce(level):
        arrive(level, (3, 0))
        gain = down_rows(pp_all[level, 0:1, :], mid)
        for at in range(chans // mid):
            cut = slice(at * mid, (at + 1) * mid)
            high, low = split(wr_all[level, :, cut] * gain)
            w_red[level, 0:mid, cut] = high
            w_red[level, mid : 2 * mid, cut] = low
        b_red[level] = down_rows(pp_all[level, 2:3, :], mid)

    def prepare_rest(level):
        arrive(level, (1, 2))
        gain = down_rows(pp_all[level, 1:2, :], mid)
        for tap in range(9):
            p, q = tap // 3, tap % 3
            high, low = split(ws_all[level, tap] * gain)
            w_spa[p, 0:mid, q * mid : (q + 1) * mid] = high
            w_spa[p, mid : 2 * mid, q * mid : (q + 1) * mid] = low
        b_mid[...] = down_rows(pp_all[level, 3:4, :], mid)
        count = chans // mid
        for at in range(count):
            cut = slice(at * mid, (at + 1) * mid)
            high, low = split(wx_all[level, cut, :] * down_rows(pp_all[level, 4 + at : 5 + at, :], mid))
            w_exp[cut, 0:mid] = high
            w_exp[cut, mid : 2 * mid] = high
            w_exp[cut, 2 * mid : 3 * mid] = low
            b_out[cut, :] = down_rows(pp_all[level, 4 + count + at : 5 + count + at, :], mid)

    def to_strip(level, m, way):
        return remote(
            red.at[level, m, rows - 1 if way == 0 else 0], halo.at[level, m, way],
            hsend.at[level, m, way], hrecv.at[level, m, way],
            {"strip": strip + 1 if way == 0 else strip - 1},
        )

    def to_side(level, m):
        return remote(red.at[level, m], side.at[level, m], nsend.at[level, m], nrecv.at[level, m], other)

    def pass_on(level, m, way):
        return remote(
            halo.at[level, m, way], relay.at[level, m, way],
            ysend.at[level, m, way], yrecv.at[level, m, way], other,
        )

    has = (strip > 0, strip < strips - 1)

    def reduce_tile(level, m):
        weights = w_red[level]
        bias = b_red[level]
        for pair in range(rows // 2):
            parts = [
                split(cur.at[m][pl.ds(2 * pair + j, chans, stride=rows), :]) for j in range(2)
            ]
            high = jnp.concatenate([part[0] for part in parts], axis=1)
            low = jnp.concatenate([part[1] for part in parts], axis=1)
            both = dot(weights, high)
            total = both[:mid] + both[mid:] + dot(weights[:mid], low)
            for j in range(2):
                red[level, m, 2 * pair + j] = jnp.maximum(total[:, j * cols : (j + 1) * cols] + bias, 0.0)

        @pl.when(has[1])
        def _():
            to_strip(level, m, 0).start()

        @pl.when(has[0])
        def _():
            to_strip(level, m, 1).start()

        to_side(level, m).start()

    def take_halo(level, m):
        for way in range(2):
            @pl.when(has[way])
            def _(way=way):
                to_strip(level, m, way).wait_recv()
                pass_on(level, m, way).start()

    lane = lax.broadcasted_iota(jnp.int32, (mid, cols), 1)
    left_edge = lane == cols - 1
    right_edge = lane == 0
    left_on = jnp.where(col == 1, 1.0, 0.0).astype(F32)
    right_on = jnp.where(col == 0, 1.0, 0.0).astype(F32)

    def finish_tile(level, m):
        to_side(level, m).wait_recv()
        for way in range(2):
            @pl.when(has[way])
            def _(way=way):
                pass_on(level, m, way).wait_recv()
        for at in range(rows + 2):
            if at == 0:
                centre, beside = halo[level, m, 0], relay[level, m, 0]
            elif at == rows + 1:
                centre, beside = halo[level, m, 1], relay[level, m, 1]
            else:
                centre, beside = red[level, m, at - 1], side[level, m, at - 1]
            lanes = slice(at * cols, (at + 1) * cols)
            left = pltpu.roll(jnp.where(left_edge, beside * left_on, centre), 1, 1)
            right = pltpu.roll(jnp.where(right_edge, beside * right_on, centre), cols - 1, 1)
            for q, value in enumerate((left, centre, right)):
                high, low = split(value)
                sa[q * mid : (q + 1) * mid, lanes] = high
                sa[(3 + q) * mid : (4 + q) * mid, lanes] = low
        bias = b_mid[...]
        for pair in range(rows // 2):
            both = jnp.zeros((2 * mid, 2 * cols), F32)
            one = jnp.zeros((mid, 2 * cols), F32)
            for p in range(3):
                lanes = slice((2 * pair + p) * cols, (2 * pair + p + 2) * cols)
                both = both + dot(w_spa[p], sa[0 : 3 * mid, lanes])
                one = one + dot(w_spa[p, 0:mid, :], sa[3 * mid : 6 * mid, lanes])
            total = both[:mid] + both[mid:] + one
            total = jnp.maximum(total + jnp.concatenate([bias, bias], axis=1), 0.0)
            high, low = split(total)
            stack = jnp.concatenate([high, low, high], axis=0)
            grown = dot(w_exp[...], stack)
            for j in range(2):
                at = pl.ds(2 * pair + j, chans, stride=rows)
                cur.at[m][at, :] = jnp.maximum(
                    cur.at[m][at, :] + grown[:, j * cols : (j + 1) * cols] + b_out[...], 0.0
                )

    def store(m):
        return pltpu.make_async_copy(cur.at[m], out_ref.at[m], out_sem.at[m])

    prepare_reduce(0)

    @pl.loop(0, tiles)
    def _(m):
        pltpu.make_async_copy(x_ref.at[m], cur.at[m], x_sem.at[m]).wait()
        reduce_tile(0, m)

    for level in range(levels):
        @pl.when(sec >= level)
        def _(level=level):
            prepare_rest(level)
            if level + 1 < levels:
                @pl.when(sec > level)
                def _():
                    prepare_reduce(level + 1)

            take_halo(level, 0)

            @pl.loop(0, tiles)
            def _(m):
                @pl.when(m + 1 < tiles)
                def _():
                    take_halo(level, m + 1)

                finish_tile(level, m)
                if level + 1 < levels:
                    @pl.when(sec > level)
                    def _():
                        reduce_tile(level + 1, m)

                @pl.when(sec == level)
                def _():
                    store(m).start()

            @pl.loop(0, tiles)
            def _(m):
                to_side(level, m).wait_send()
                for way in range(2):
                    @pl.when(has[1 - way])
                    def _(way=way):
                        to_strip(level, m, way).wait_send()

                    @pl.when(has[way])
                    def _(way=way):
                        pass_on(level, m, way).wait_send()

                @pl.when(sec == level)
                def _():
                    store(m).wait()

    for k in range(4):
        for target in range(1, levels):
            @pl.when(sec < target)
            def _(k=k, target=target):
                part = share(k, sec, col)
                remote(part, part, wsend.at[k, target], wrecv.at[k, sec], {"section": target}).wait_send()
        if k < 3:
            for level in range(levels - 1):
                @pl.when(sec > level)
                def _(k=k, level=level):
                    relayed(k, level, col).wait_send()


def on_device(levels, strips, x_in, w_reduce, w_spatial, w_expand, gain_mid, bias_mid, gain_out, bias_out):
    tiles, chans, rows, cols = x_in.shape
    mid = w_reduce.shape[1]
    terms = jnp.concatenate(
        [
            gain_mid[0], bias_mid[0],
            gain_out.reshape(chans // mid, mid), bias_out.reshape(chans // mid, mid),
            jnp.zeros((4, mid), F32),
        ],
        axis=0,
    )
    dma = pltpu.SemaphoreType.DMA
    out = pl.pallas_call(
        functools.partial(kernel, levels, strips, rows),
        out_shape=jax.ShapeDtypeStruct((tiles, chans * rows, cols), F32),
        in_specs=[pl.BlockSpec(memory_space=pl.ANY)] * 5,
        out_specs=pl.BlockSpec(memory_space=pl.ANY),
        scratch_shapes=[
            pltpu.VMEM((tiles, chans * rows, cols), F32),
            pltpu.VMEM((levels, mid, chans), F32),
            pltpu.VMEM((levels, 9, mid, mid), F32),
            pltpu.VMEM((levels, chans, mid), F32),
            pltpu.VMEM((levels,) + terms.shape, F32),
            pltpu.VMEM((levels, tiles, rows, mid, cols), F32),
            pltpu.VMEM((levels, tiles, rows, mid, cols), F32),
            pltpu.VMEM((levels, tiles, 2, mid, cols), F32),
            pltpu.VMEM((levels, tiles, 2, mid, cols), F32),
            pltpu.VMEM((levels, 2 * mid, chans), BF),
            pltpu.VMEM((3, 2 * mid, 3 * mid), BF),
            pltpu.VMEM((chans, 3 * mid), BF),
            pltpu.VMEM((levels, mid, cols), F32),
            pltpu.VMEM((mid, cols), F32),
            pltpu.VMEM((chans, cols), F32),
            pltpu.VMEM((6 * mid, (rows + 2) * cols), BF),
            dma((tiles,)),
            dma((4,)),
            dma((4, levels)),
            dma((4, levels)),
            dma((3, levels)),
            dma((3, levels)),
            dma((levels, tiles, 2)),
            dma((levels, tiles, 2)),
            dma((levels, tiles)),
            dma((levels, tiles)),
            dma((levels, tiles, 2)),
            dma((levels, tiles, 2)),
            dma((tiles,)),
        ],
        compiler_params=pltpu.CompilerParams(
            collective_id=0, has_side_effects=True, vmem_limit_bytes=60 * 1024 * 1024
        ),
        name="blocks",
    )(x_in.reshape(tiles, chans * rows, cols), w_reduce[0], w_spatial[0], w_expand[0], terms)
    return out.reshape(1, tiles, chans, rows, cols)


def solution(mesh):
    in_specs = (
        P("groups", None, "strip", "col"),
        P("section", None, None),
        P("section", None, None, None),
        P("section", None, None),
        P("section", None, None),
        P("section", None, None),
        P("section", None),
        P("section", None),
    )
    out_specs = P("section", "groups", None, "strip", "col")
    return jax.shard_map(
        functools.partial(on_device, mesh.shape["section"], mesh.shape["strip"]),
        mesh=mesh, in_specs=in_specs, out_specs=out_specs, check_vma=False,
    )
```

```python
import functools

import jax
import jax.numpy as jnp
from jax import lax
from jax.experimental import pallas as pl
from jax.experimental.pallas import tpu as pltpu
from jax.sharding import PartitionSpec as P

BF = jnp.bfloat16
F32 = jnp.float32


def split(value):
    high = value.astype(BF)
    return high, (value - high.astype(F32)).astype(BF)


def dot(a, b):
    return jnp.dot(a, b, preferred_element_type=F32)


def down_rows(row, size):
    return jnp.transpose(jnp.broadcast_to(row, (size, size)))


def kernel(
    levels, strips, rows,
    x_ref, wr_ref, ws_ref, wx_ref, gm_ref, bm_ref, go_ref, bo_ref, out_ref,
    cur, wr_all, ws_all, wx_all, gm_all, bm_all, go_all, bo_all, red, side, halo, relay,
    w_red, w_spa, w_exp, b_red, b_mid, b_out, sa,
    x_sem, own_sem, wsend, wrecv, rsend, rrecv, gsend, grecv, hsend, hrecv, nsend, nrecv, ysend, yrecv, out_sem,
):
    tiles = x_ref.shape[0]
    chans = x_ref.shape[1] // rows
    cols = x_ref.shape[2]
    mid = wr_ref.shape[0]
    strip = lax.axis_index("strip")
    sec = lax.axis_index("section")
    col = lax.axis_index("col")
    group = lax.axis_index("groups")
    other = {"col": 1 - col}
    across = {"groups": 1 - group}
    srcs = (wr_ref, ws_ref, wx_ref, gm_ref, bm_ref, go_ref, bo_ref)
    slots = (wr_all, ws_all, wx_all, gm_all, bm_all, go_all, bo_all)
    kinds = len(srcs)
    order = (3, 4, 5, 6, 0, 1, 2)

    def cut(kind, level, parts, which):
        if kind == 0:
            return wr_all.at[level, pl.ds(which * (mid // parts), mid // parts), :]
        if kind == 1:
            return ws_all.at[level, :, pl.ds(which * (mid // parts), mid // parts), :]
        if kind == 2:
            return wx_all.at[level, pl.ds(which * (chans // parts), chans // parts), :]
        return slots[kind].at[level]

    def share(kind, level):
        if kind == 0:
            return cut(kind, level, 2, col)
        return cut(kind, level, 4, 2 * col + group)

    def remote(src, dst, send, recv, device):
        return pltpu.make_async_remote_copy(
            src_ref=src, dst_ref=dst, send_sem=send, recv_sem=recv,
            device_id=device, device_id_type=pl.DeviceIdType.MESH,
        )

    own = [
        pltpu.make_async_copy(srcs[k], slots[k].at[sec], own_sem.at[k]) for k in range(kinds)
    ]
    loads = [
        pltpu.make_async_copy(x_ref.at[m], cur.at[m], x_sem.at[m]) for m in range(tiles)
    ]
    for k in order:
        own[k].start()
    for copy in loads:
        copy.start()

    barrier = pltpu.get_barrier_semaphore()
    pl.semaphore_signal(barrier, inc=1, device_id=other, device_id_type=pl.DeviceIdType.MESH)
    pl.semaphore_signal(barrier, inc=1, device_id=across, device_id_type=pl.DeviceIdType.MESH)
    for step in range(1, levels):
        pl.semaphore_signal(
            barrier, inc=1, device_id={"section": lax.rem(sec + step, levels)},
            device_id_type=pl.DeviceIdType.MESH,
        )

    for there, peer in ((strip > 0, strip - 1), (strip < strips - 1, strip + 1)):
        @pl.when(there)
        def _(peer=peer):
            pl.semaphore_signal(
                barrier, inc=1, device_id={"strip": peer}, device_id_type=pl.DeviceIdType.MESH
            )

    peers = levels + 1 + jnp.where(strip > 0, 1, 0) + jnp.where(strip < strips - 1, 1, 0)
    pl.semaphore_wait(barrier, peers)

    for k in order:
        own[k].wait()
        for target in range(1, levels):
            @pl.when(sec < target)
            def _(k=k, target=target):
                part = share(k, sec)
                remote(part, part, wsend.at[k, target], wrecv.at[k, sec], {"section": target}).start()

    @pl.when(strip == 0)
    def _():
        halo[:, :, 0] = jnp.zeros(halo.shape[:2] + halo.shape[3:], F32)
        relay[:, :, 0] = jnp.zeros(relay.shape[:2] + relay.shape[3:], F32)

    @pl.when(strip == strips - 1)
    def _():
        halo[:, :, 1] = jnp.zeros(halo.shape[:2] + halo.shape[3:], F32)
        relay[:, :, 1] = jnp.zeros(relay.shape[:2] + relay.shape[3:], F32)

    def relayed(k, level, which):
        part = cut(k, level, 2, which)
        return remote(part, part, rsend.at[k, level], rrecv.at[k, level], other)

    def crossed(k, level, which):
        part = cut(k, level, 4, 2 * col + which)
        return remote(part, part, gsend.at[k, level], grecv.at[k, level], across)

    def arrived(k, level):
        part = share(k, level)
        remote(part, part, wsend.at[k, 0], wrecv.at[k, level], other).wait_recv()

    def step_one(level, k):
        @pl.when(sec > level)
        def _():
            arrived(k, level)
            crossed(k, level, group).start()

    def step_two(level, k):
        @pl.when(sec > level)
        def _():
            crossed(k, level, 1 - group).wait_recv()
            relayed(k, level, col).start()

    def step_three(level, k):
        @pl.when(sec > level)
        def _():
            relayed(k, level, 1 - col).wait_recv()

    def arrive_reduce(level):
        @pl.when(sec > level)
        def _():
            arrived(0, level)
            relayed(0, level, col).start()
            for k in range(3, kinds):
                arrived(k, level)
            relayed(0, level, 1 - col).wait_recv()

    def prepare_reduce(level):
        arrive_reduce(level)
        gain = down_rows(gm_all[level, 0:1, :], mid)
        for at in range(chans // mid):
            chunk = slice(at * mid, (at + 1) * mid)
            high, low = split(wr_all[level, :, chunk] * gain)
            w_red[level, 0:mid, chunk] = high
            w_red[level, mid : 2 * mid, chunk] = low
        b_red[level] = down_rows(bm_all[level, 0:1, :], mid)

    def prepare_rest(level):
        if level > 0:
            for step in (step_one, step_two):
                step(level, 1)
                step(level, 2)
        step_three(level, 1)
        gain = down_rows(gm_all[level, 1:2, :], mid)
        for tap in range(9):
            p, q = tap // 3, tap % 3
            high, low = split(ws_all[level, tap] * gain)
            w_spa[p, 0:mid, q * mid : (q + 1) * mid] = high
            w_spa[p, mid : 2 * mid, q * mid : (q + 1) * mid] = low
        b_mid[...] = down_rows(bm_all[level, 1:2, :], mid)
        step_three(level, 2)
        for at in range(chans // mid):
            chunk = slice(at * mid, (at + 1) * mid)
            high, low = split(wx_all[level, chunk, :] * down_rows(go_all[level, :, chunk], mid))
            w_exp[chunk, 0:mid] = high
            w_exp[chunk, mid : 2 * mid] = high
            w_exp[chunk, 2 * mid : 3 * mid] = low
            b_out[chunk, :] = down_rows(bo_all[level, :, chunk], mid)

    def to_strip(level, m, way):
        return remote(
            red.at[level, m, rows - 1 if way == 0 else 0], halo.at[level, m, way],
            hsend.at[level, m, way], hrecv.at[level, m, way],
            {"strip": strip + 1 if way == 0 else strip - 1},
        )

    def to_side(level, m):
        return remote(red.at[level, m], side.at[level, m], nsend.at[level, m], nrecv.at[level, m], other)

    def pass_on(level, m, way):
        return remote(
            halo.at[level, m, way], relay.at[level, m, way],
            ysend.at[level, m, way], yrecv.at[level, m, way], other,
        )

    has = (strip > 0, strip < strips - 1)

    def reduce_tile(level, m):
        weights = w_red[level]
        bias = b_red[level]
        for pair in range(rows // 2):
            parts = [
                split(cur.at[m][pl.ds(2 * pair + j, chans, stride=rows), :]) for j in range(2)
            ]
            high = jnp.concatenate([part[0] for part in parts], axis=1)
            low = jnp.concatenate([part[1] for part in parts], axis=1)
            both = dot(weights, high)
            total = both[:mid] + both[mid:] + dot(weights[:mid], low)
            for j in range(2):
                red[level, m, 2 * pair + j] = jnp.maximum(total[:, j * cols : (j + 1) * cols] + bias, 0.0)

        @pl.when(has[1])
        def _():
            to_strip(level, m, 0).start()

        @pl.when(has[0])
        def _():
            to_strip(level, m, 1).start()

        to_side(level, m).start()

    def take_halo(level, m):
        for way in range(2):
            @pl.when(has[way])
            def _(way=way):
                to_strip(level, m, way).wait_recv()
                pass_on(level, m, way).start()

    lane = lax.broadcasted_iota(jnp.int32, (mid, cols), 1)
    left_edge = lane == cols - 1
    right_edge = lane == 0
    left_on = jnp.where(col == 1, 1.0, 0.0).astype(F32)
    right_on = jnp.where(col == 0, 1.0, 0.0).astype(F32)

    def finish_tile(level, m):
        to_side(level, m).wait_recv()
        for way in range(2):
            @pl.when(has[way])
            def _(way=way):
                pass_on(level, m, way).wait_recv()
        for at in range(rows + 2):
            if at == 0:
                centre, beside = halo[level, m, 0], relay[level, m, 0]
            elif at == rows + 1:
                centre, beside = halo[level, m, 1], relay[level, m, 1]
            else:
                centre, beside = red[level, m, at - 1], side[level, m, at - 1]
            lanes = slice(at * cols, (at + 1) * cols)
            left = pltpu.roll(jnp.where(left_edge, beside * left_on, centre), 1, 1)
            right = pltpu.roll(jnp.where(right_edge, beside * right_on, centre), cols - 1, 1)
            for q, value in enumerate((left, centre, right)):
                high, low = split(value)
                sa[q * mid : (q + 1) * mid, lanes] = high
                sa[(3 + q) * mid : (4 + q) * mid, lanes] = low
        bias = b_mid[...]
        for pair in range(rows // 2):
            both = jnp.zeros((2 * mid, 2 * cols), F32)
            one = jnp.zeros((mid, 2 * cols), F32)
            for p in range(3):
                lanes = slice((2 * pair + p) * cols, (2 * pair + p + 2) * cols)
                both = both + dot(w_spa[p], sa[0 : 3 * mid, lanes])
                one = one + dot(w_spa[p, 0:mid, :], sa[3 * mid : 6 * mid, lanes])
            total = both[:mid] + both[mid:] + one
            total = jnp.maximum(total + jnp.concatenate([bias, bias], axis=1), 0.0)
            high, low = split(total)
            stack = jnp.concatenate([high, low, high], axis=0)
            grown = dot(w_exp[...], stack)
            for j in range(2):
                at = pl.ds(2 * pair + j, chans, stride=rows)
                cur.at[m][at, :] = jnp.maximum(
                    cur.at[m][at, :] + grown[:, j * cols : (j + 1) * cols] + b_out[...], 0.0
                )

    def store(m):
        return pltpu.make_async_copy(cur.at[m], out_ref.at[m], out_sem.at[m])

    prepare_reduce(0)
    if levels > 1:
        step_one(0, 1)

    @pl.loop(0, tiles)
    def _(m):
        pltpu.make_async_copy(x_ref.at[m], cur.at[m], x_sem.at[m]).wait()
        reduce_tile(0, m)
        if levels > 1:
            @pl.when(m == tiles // 2 - 1)
            def _():
                step_one(0, 2)
                step_two(0, 1)

    if levels > 1:
        step_two(0, 2)

    for level in range(levels):
        @pl.when(sec >= level)
        def _(level=level):
            prepare_rest(level)
            if level + 1 < levels:
                @pl.when(sec > level)
                def _():
                    prepare_reduce(level + 1)

            take_halo(level, 0)

            @pl.loop(0, tiles)
            def _(m):
                @pl.when(m + 1 < tiles)
                def _():
                    take_halo(level, m + 1)

                finish_tile(level, m)
                if level + 1 < levels:
                    @pl.when(sec > level)
                    def _():
                        reduce_tile(level + 1, m)

                @pl.when(sec == level)
                def _():
                    store(m).start()

            @pl.loop(0, tiles)
            def _(m):
                to_side(level, m).wait_send()
                for way in range(2):
                    @pl.when(has[1 - way])
                    def _(way=way):
                        to_strip(level, m, way).wait_send()

                    @pl.when(has[way])
                    def _(way=way):
                        pass_on(level, m, way).wait_send()

                @pl.when(sec == level)
                def _():
                    store(m).wait()

    for k in range(kinds):
        for target in range(1, levels):
            @pl.when(sec < target)
            def _(k=k, target=target):
                part = share(k, sec)
                remote(part, part, wsend.at[k, target], wrecv.at[k, sec], {"section": target}).wait_send()
        if k < 3:
            for level in range(levels - 1):
                @pl.when(sec > level)
                def _(k=k, level=level):
                    relayed(k, level, col).wait_send()
                    if k > 0:
                        crossed(k, level, group).wait_send()


def emit(in_ref, out_ref, sems):
    copies = [
        pltpu.make_async_copy(in_ref.at[m], out_ref.at[m], sems.at[m]) for m in range(in_ref.shape[0])
    ]
    for copy in copies:
        copy.start()
    for copy in copies:
        copy.wait()


def on_device(levels, strips, x_in, w_reduce, w_spatial, w_expand, gain_mid, bias_mid, gain_out, bias_out):
    tiles, chans, rows, cols = x_in.shape
    mid = w_reduce.shape[1]
    dma = pltpu.SemaphoreType.DMA
    out = pl.pallas_call(
        functools.partial(kernel, levels, strips, rows),
        out_shape=jax.ShapeDtypeStruct((tiles, chans * rows, cols), F32),
        in_specs=[pl.BlockSpec(memory_space=pltpu.HBM)] * 8,
        out_specs=pl.BlockSpec(memory_space=pl.ANY),
        scratch_shapes=[
            pltpu.VMEM((tiles, chans * rows, cols), F32),
            pltpu.VMEM((levels, mid, chans), F32),
            pltpu.VMEM((levels, 9, mid, mid), F32),
            pltpu.VMEM((levels, chans, mid), F32),
            pltpu.VMEM((levels,) + gain_mid.shape[1:], F32),
            pltpu.VMEM((levels,) + bias_mid.shape[1:], F32),
            pltpu.VMEM((levels,) + gain_out.shape, F32),
            pltpu.VMEM((levels,) + bias_out.shape, F32),
            pltpu.VMEM((levels, tiles, rows, mid, cols), F32),
            pltpu.VMEM((levels, tiles, rows, mid, cols), F32),
            pltpu.VMEM((levels, tiles, 2, mid, cols), F32),
            pltpu.VMEM((levels, tiles, 2, mid, cols), F32),
            pltpu.VMEM((levels, 2 * mid, chans), BF),
            pltpu.VMEM((3, 2 * mid, 3 * mid), BF),
            pltpu.VMEM((chans, 3 * mid), BF),
            pltpu.VMEM((levels, mid, cols), F32),
            pltpu.VMEM((mid, cols), F32),
            pltpu.VMEM((chans, cols), F32),
            pltpu.VMEM((6 * mid, (rows + 2) * cols), BF),
            dma((tiles,)),
            dma((7,)),
            dma((7, levels)),
            dma((7, levels)),
            dma((3, levels)),
            dma((3, levels)),
            dma((3, levels)),
            dma((3, levels)),
            dma((levels, tiles, 2)),
            dma((levels, tiles, 2)),
            dma((levels, tiles)),
            dma((levels, tiles)),
            dma((levels, tiles, 2)),
            dma((levels, tiles, 2)),
            dma((tiles,)),
        ],
        compiler_params=pltpu.CompilerParams(
            collective_id=0, has_side_effects=True, vmem_limit_bytes=40 * 1024 * 1024
        ),
        name="blocks",
    )(x_in.reshape(tiles, chans * rows, cols), w_reduce[0], w_spatial[0], w_expand[0], gain_mid[0], bias_mid[0], gain_out, bias_out)
    out = pl.pallas_call(
        emit,
        out_shape=jax.ShapeDtypeStruct(out.shape, F32),
        in_specs=[pl.BlockSpec(memory_space=pltpu.VMEM)],
        out_specs=pl.BlockSpec(memory_space=pltpu.HBM),
        scratch_shapes=[dma((tiles,))],
        compiler_params=pltpu.CompilerParams(vmem_limit_bytes=16 * 1024 * 1024),
        name="emit",
    )(out)
    return out.reshape(1, tiles, chans, rows, cols)


def solution(mesh):
    in_specs = (
        P("groups", None, "strip", "col"),
        P("section", None, None),
        P("section", None, None, None),
        P("section", None, None),
        P("section", None, None),
        P("section", None, None),
        P("section", None),
        P("section", None),
    )
    out_specs = P("section", "groups", None, "strip", "col")
    return jax.shard_map(
        functools.partial(on_device, mesh.shape["section"], mesh.shape["strip"]),
        mesh=mesh, in_specs=in_specs, out_specs=out_specs, check_vma=False,
    )
```

```python
import functools

import jax
import jax.numpy as jnp
from jax import lax
from jax.experimental import pallas as pl
from jax.experimental.pallas import tpu as pltpu
from jax.sharding import PartitionSpec as P

BF = jnp.bfloat16
F32 = jnp.float32


def split(value):
    high = value.astype(BF)
    return high, (value - high.astype(F32)).astype(BF)


def dot(a, b):
    return jnp.dot(a, b, preferred_element_type=F32)


def down_rows(row, size):
    return jnp.transpose(jnp.broadcast_to(row, (size, size)))


def kernel(
    levels, strips, rows,
    x_ref, wr_ref, ws_ref, wx_ref, gm_ref, bm_ref, go_ref, bo_ref, out_ref,
    cur, wr_all, ws_all, wx_all, gm_all, bm_all, go_all, bo_all, red, side, halo, relay,
    w_red, w_spa, w_exp, b_red, b_mid, b_out, sa,
    x_sem, own_sem, wsend, wrecv, rsend, rrecv, gsend, grecv, hsend, hrecv, nsend, nrecv, ysend, yrecv, out_sem,
):
    tiles = x_ref.shape[0]
    chans = x_ref.shape[1] // rows
    cols = x_ref.shape[2]
    mid = wr_ref.shape[0]
    strip = lax.axis_index("strip")
    sec = lax.axis_index("section")
    col = lax.axis_index("col")
    group = lax.axis_index("groups")
    other = {"col": 1 - col}
    across = {"groups": 1 - group}
    srcs = (wr_ref, ws_ref, wx_ref, gm_ref, bm_ref, go_ref, bo_ref)
    slots = (wr_all, ws_all, wx_all, gm_all, bm_all, go_all, bo_all)
    kinds = len(srcs)
    order = (3, 4, 5, 6, 0, 1, 2)

    def cut(kind, level, parts, which):
        if kind == 0:
            return wr_all.at[level, pl.ds(which * (mid // parts), mid // parts), :]
        if kind == 1:
            return ws_all.at[level, :, pl.ds(which * (mid // parts), mid // parts), :]
        if kind == 2:
            return wx_all.at[level, pl.ds(which * (chans // parts), chans // parts), :]
        return slots[kind].at[level]

    def share(kind, level):
        if kind == 0:
            return cut(kind, level, 2, col)
        return cut(kind, level, 4, 2 * col + group)

    def remote(src, dst, send, recv, device):
        return pltpu.make_async_remote_copy(
            src_ref=src, dst_ref=dst, send_sem=send, recv_sem=recv,
            device_id=device, device_id_type=pl.DeviceIdType.MESH,
        )

    own = [
        pltpu.make_async_copy(srcs[k], slots[k].at[sec], own_sem.at[k]) for k in range(kinds)
    ]
    loads = [
        pltpu.make_async_copy(x_ref.at[m], cur.at[m], x_sem.at[m]) for m in range(tiles)
    ]
    for k in order:
        own[k].start()
    for copy in loads:
        copy.start()

    barrier = pltpu.get_barrier_semaphore()
    pl.semaphore_signal(barrier, inc=1, device_id=other, device_id_type=pl.DeviceIdType.MESH)
    pl.semaphore_signal(barrier, inc=1, device_id=across, device_id_type=pl.DeviceIdType.MESH)
    for step in range(1, levels):
        pl.semaphore_signal(
            barrier, inc=1, device_id={"section": lax.rem(sec + step, levels)},
            device_id_type=pl.DeviceIdType.MESH,
        )

    for there, peer in ((strip > 0, strip - 1), (strip < strips - 1, strip + 1)):
        @pl.when(there)
        def _(peer=peer):
            pl.semaphore_signal(
                barrier, inc=1, device_id={"strip": peer}, device_id_type=pl.DeviceIdType.MESH
            )

    peers = levels + 1 + jnp.where(strip > 0, 1, 0) + jnp.where(strip < strips - 1, 1, 0)
    pl.semaphore_wait(barrier, peers)

    for k in order:
        own[k].wait()
        for target in range(1, levels):
            @pl.when(sec < target)
            def _(k=k, target=target):
                part = share(k, sec)
                remote(part, part, wsend.at[k, target], wrecv.at[k, sec], {"section": target}).start()

    @pl.when(strip == 0)
    def _():
        halo[:, :, 0] = jnp.zeros(halo.shape[:2] + halo.shape[3:], F32)
        relay[:, :, 0] = jnp.zeros(relay.shape[:2] + relay.shape[3:], F32)

    @pl.when(strip == strips - 1)
    def _():
        halo[:, :, 1] = jnp.zeros(halo.shape[:2] + halo.shape[3:], F32)
        relay[:, :, 1] = jnp.zeros(relay.shape[:2] + relay.shape[3:], F32)

    def relayed(k, level, which):
        part = cut(k, level, 2, which)
        return remote(part, part, rsend.at[k, level], rrecv.at[k, level], other)

    def crossed(k, level, which):
        part = cut(k, level, 4, 2 * col + which)
        return remote(part, part, gsend.at[k, level], grecv.at[k, level], across)

    def arrived(k, level):
        part = share(k, level)
        remote(part, part, wsend.at[k, 0], wrecv.at[k, level], other).wait_recv()

    def step_one(level, k):
        @pl.when(sec > level)
        def _():
            arrived(k, level)
            crossed(k, level, group).start()

    def step_two(level, k):
        @pl.when(sec > level)
        def _():
            crossed(k, level, 1 - group).wait_recv()
            relayed(k, level, col).start()

    def step_three(level, k):
        @pl.when(sec > level)
        def _():
            relayed(k, level, 1 - col).wait_recv()

    def arrive_reduce(level):
        @pl.when(sec > level)
        def _():
            arrived(0, level)
            relayed(0, level, col).start()
            for k in range(3, kinds):
                arrived(k, level)
            relayed(0, level, 1 - col).wait_recv()

    def prepare_reduce(level):
        arrive_reduce(level)
        gain = down_rows(gm_all[level, 0:1, :], mid)
        for at in range(chans // mid):
            chunk = slice(at * mid, (at + 1) * mid)
            high, low = split(wr_all[level, :, chunk] * gain)
            w_red[level, 0:mid, chunk] = high
            w_red[level, mid : 2 * mid, chunk] = low
        b_red[level] = down_rows(bm_all[level, 0:1, :], mid)

    def prepare_rest(level):
        if level > 0:
            for step in (step_one, step_two):
                step(level, 1)
                step(level, 2)
        step_three(level, 1)
        gain = down_rows(gm_all[level, 1:2, :], mid)
        for tap in range(9):
            p, q = tap // 3, tap % 3
            high, low = split(ws_all[level, tap] * gain)
            w_spa[p, 0:mid, q * mid : (q + 1) * mid] = high
            w_spa[p, mid : 2 * mid, q * mid : (q + 1) * mid] = low
        b_mid[...] = down_rows(bm_all[level, 1:2, :], mid)
        step_three(level, 2)
        for at in range(chans // mid):
            chunk = slice(at * mid, (at + 1) * mid)
            high, low = split(wx_all[level, chunk, :] * down_rows(go_all[level, :, chunk], mid))
            w_exp[chunk, 0:mid] = high
            w_exp[chunk, mid : 2 * mid] = high
            w_exp[chunk, 2 * mid : 3 * mid] = low
            b_out[chunk, :] = down_rows(bo_all[level, :, chunk], mid)

    def to_strip(level, m, way):
        return remote(
            red.at[level, m, rows - 1 if way == 0 else 0], halo.at[level, m, way],
            hsend.at[level, m, way], hrecv.at[level, m, way],
            {"strip": strip + 1 if way == 0 else strip - 1},
        )

    def to_side(level, m):
        return remote(red.at[level, m], side.at[level, m], nsend.at[level, m], nrecv.at[level, m], other)

    def pass_on(level, m, way):
        return remote(
            halo.at[level, m, way], relay.at[level, m, way],
            ysend.at[level, m, way], yrecv.at[level, m, way], other,
        )

    has = (strip > 0, strip < strips - 1)

    def reduce_tile(level, m):
        weights = w_red[level]
        bias = b_red[level]
        for pair in range(rows // 2):
            parts = [
                split(cur.at[m][pl.ds(2 * pair + j, chans, stride=rows), :]) for j in range(2)
            ]
            high = jnp.concatenate([part[0] for part in parts], axis=1)
            low = jnp.concatenate([part[1] for part in parts], axis=1)
            both = dot(weights, high)
            total = both[:mid] + both[mid:] + dot(weights[:mid], low)
            for j in range(2):
                red[level, m, 2 * pair + j] = jnp.maximum(total[:, j * cols : (j + 1) * cols] + bias, 0.0)

        @pl.when(has[1])
        def _():
            to_strip(level, m, 0).start()

        @pl.when(has[0])
        def _():
            to_strip(level, m, 1).start()

        to_side(level, m).start()

    def take_halo(level, m):
        for way in range(2):
            @pl.when(has[way])
            def _(way=way):
                to_strip(level, m, way).wait_recv()
                pass_on(level, m, way).start()

    lane = lax.broadcasted_iota(jnp.int32, (mid, cols), 1)
    left_edge = lane == cols - 1
    right_edge = lane == 0
    left_on = jnp.where(col == 1, 1.0, 0.0).astype(F32)
    right_on = jnp.where(col == 0, 1.0, 0.0).astype(F32)

    def finish_tile(level, m):
        to_side(level, m).wait_recv()
        for way in range(2):
            @pl.when(has[way])
            def _(way=way):
                pass_on(level, m, way).wait_recv()
        for at in range(rows + 2):
            if at == 0:
                centre, beside = halo[level, m, 0], relay[level, m, 0]
            elif at == rows + 1:
                centre, beside = halo[level, m, 1], relay[level, m, 1]
            else:
                centre, beside = red[level, m, at - 1], side[level, m, at - 1]
            lanes = slice(at * cols, (at + 1) * cols)
            left = pltpu.roll(jnp.where(left_edge, beside * left_on, centre), 1, 1)
            right = pltpu.roll(jnp.where(right_edge, beside * right_on, centre), cols - 1, 1)
            for q, value in enumerate((left, centre, right)):
                high, low = split(value)
                sa[q * mid : (q + 1) * mid, lanes] = high
                sa[(3 + q) * mid : (4 + q) * mid, lanes] = low
        bias = b_mid[...]
        for pair in range(rows // 2):
            both = jnp.zeros((2 * mid, 2 * cols), F32)
            one = jnp.zeros((mid, 2 * cols), F32)
            for p in range(3):
                lanes = slice((2 * pair + p) * cols, (2 * pair + p + 2) * cols)
                both = both + dot(w_spa[p], sa[0 : 3 * mid, lanes])
                one = one + dot(w_spa[p, 0:mid, :], sa[3 * mid : 6 * mid, lanes])
            total = both[:mid] + both[mid:] + one
            total = jnp.maximum(total + jnp.concatenate([bias, bias], axis=1), 0.0)
            high, low = split(total)
            stack = jnp.concatenate([high, low, high], axis=0)
            grown = dot(w_exp[...], stack)
            for j in range(2):
                at = pl.ds(2 * pair + j, chans, stride=rows)
                cur.at[m][at, :] = jnp.maximum(
                    cur.at[m][at, :] + grown[:, j * cols : (j + 1) * cols] + b_out[...], 0.0
                )

    def store(m):
        return pltpu.make_async_copy(cur.at[m], out_ref.at[m], out_sem.at[m])

    prepare_reduce(0)
    if levels > 1:
        step_one(0, 1)

    @pl.loop(0, tiles)
    def _(m):
        pltpu.make_async_copy(x_ref.at[m], cur.at[m], x_sem.at[m]).wait()
        reduce_tile(0, m)
        if levels > 1:
            @pl.when(m == tiles // 2 - 1)
            def _():
                step_one(0, 2)
                step_two(0, 1)

    if levels > 1:
        step_two(0, 2)

    for level in range(levels):
        @pl.when(sec >= level)
        def _(level=level):
            prepare_rest(level)
            if level + 1 < levels:
                @pl.when(sec > level)
                def _():
                    prepare_reduce(level + 1)

            take_halo(level, 0)

            @pl.loop(0, tiles)
            def _(m):
                @pl.when(m + 1 < tiles)
                def _():
                    take_halo(level, m + 1)

                finish_tile(level, m)
                if level + 1 < levels:
                    @pl.when(sec > level)
                    def _():
                        reduce_tile(level + 1, m)

                @pl.when(sec == level)
                def _():
                    store(m).start()

            @pl.loop(0, tiles)
            def _(m):
                to_side(level, m).wait_send()
                for way in range(2):
                    @pl.when(has[1 - way])
                    def _(way=way):
                        to_strip(level, m, way).wait_send()

                    @pl.when(has[way])
                    def _(way=way):
                        pass_on(level, m, way).wait_send()

                @pl.when(sec == level)
                def _():
                    store(m).wait()

    for k in range(kinds):
        for target in range(1, levels):
            @pl.when(sec < target)
            def _(k=k, target=target):
                part = share(k, sec)
                remote(part, part, wsend.at[k, target], wrecv.at[k, sec], {"section": target}).wait_send()
        if k < 3:
            for level in range(levels - 1):
                @pl.when(sec > level)
                def _(k=k, level=level):
                    relayed(k, level, col).wait_send()
                    if k > 0:
                        crossed(k, level, group).wait_send()


def emit(in_ref, out_ref):
    out_ref[...] = in_ref[...]


def on_device(levels, strips, x_in, w_reduce, w_spatial, w_expand, gain_mid, bias_mid, gain_out, bias_out):
    tiles, chans, rows, cols = x_in.shape
    mid = w_reduce.shape[1]
    dma = pltpu.SemaphoreType.DMA
    out = pl.pallas_call(
        functools.partial(kernel, levels, strips, rows),
        out_shape=jax.ShapeDtypeStruct((tiles, chans * rows, cols), F32),
        in_specs=[pl.BlockSpec(memory_space=pl.ANY)] * 8,
        out_specs=pl.BlockSpec(memory_space=pl.ANY),
        scratch_shapes=[
            pltpu.VMEM((tiles, chans * rows, cols), F32),
            pltpu.VMEM((levels, mid, chans), F32),
            pltpu.VMEM((levels, 9, mid, mid), F32),
            pltpu.VMEM((levels, chans, mid), F32),
            pltpu.VMEM((levels,) + gain_mid.shape[1:], F32),
            pltpu.VMEM((levels,) + bias_mid.shape[1:], F32),
            pltpu.VMEM((levels,) + gain_out.shape, F32),
            pltpu.VMEM((levels,) + bias_out.shape, F32),
            pltpu.VMEM((levels, tiles, rows, mid, cols), F32),
            pltpu.VMEM((levels, tiles, rows, mid, cols), F32),
            pltpu.VMEM((levels, tiles, 2, mid, cols), F32),
            pltpu.VMEM((levels, tiles, 2, mid, cols), F32),
            pltpu.VMEM((levels, 2 * mid, chans), BF),
            pltpu.VMEM((3, 2 * mid, 3 * mid), BF),
            pltpu.VMEM((chans, 3 * mid), BF),
            pltpu.VMEM((levels, mid, cols), F32),
            pltpu.VMEM((mid, cols), F32),
            pltpu.VMEM((chans, cols), F32),
            pltpu.VMEM((6 * mid, (rows + 2) * cols), BF),
            dma((tiles,)),
            dma((7,)),
            dma((7, levels)),
            dma((7, levels)),
            dma((3, levels)),
            dma((3, levels)),
            dma((3, levels)),
            dma((3, levels)),
            dma((levels, tiles, 2)),
            dma((levels, tiles, 2)),
            dma((levels, tiles)),
            dma((levels, tiles)),
            dma((levels, tiles, 2)),
            dma((levels, tiles, 2)),
            dma((tiles,)),
        ],
        compiler_params=pltpu.CompilerParams(
            collective_id=0, has_side_effects=True, vmem_limit_bytes=60 * 1024 * 1024
        ),
        name="blocks",
    )(x_in.reshape(tiles, chans * rows, cols), w_reduce[0], w_spatial[0], w_expand[0], gain_mid[0], bias_mid[0], gain_out, bias_out)
    half = chans * rows // 2
    out = pl.pallas_call(
        emit,
        grid=(tiles, 2),
        out_shape=jax.ShapeDtypeStruct(out.shape, F32),
        in_specs=[pl.BlockSpec((1, half, cols), lambda m, h: (m, h, 0))],
        out_specs=pl.BlockSpec((1, half, cols), lambda m, h: (m, h, 0)),
        compiler_params=pltpu.CompilerParams(vmem_limit_bytes=60 * 1024 * 1024),
        name="emit",
    )(out)
    return out.reshape(1, tiles, chans, rows, cols)


def solution(mesh):
    in_specs = (
        P("groups", None, "strip", "col"),
        P("section", None, None),
        P("section", None, None, None),
        P("section", None, None),
        P("section", None, None),
        P("section", None, None),
        P("section", None),
        P("section", None),
    )
    out_specs = P("section", "groups", None, "strip", "col")
    return jax.shard_map(
        functools.partial(on_device, mesh.shape["section"], mesh.shape["strip"]),
        mesh=mesh, in_specs=in_specs, out_specs=out_specs, check_vma=False,
    )
```
